512 devices in a mesh: blk: 64 (over x, z_hi, y), grp: 8 (over z_lo, core).
Axes of the slice: x: 4, y: 8, z: 8 (z_hi: 2, z_lo: 4; z = z_hi * 4 + z_lo), core: 2. Of those that a mesh axis runs over, the one named last changes fastest.
Arguments:
- excitation: bfloat16 [128, 1024, 256], P('blk'), may hold values from -6 to 6
- inverse_self: bfloat16 [128, 1024, 1024], P('blk', 'grp'), may hold values from -0.1875 to 0.1875
- coupling: bfloat16 [128, 4, 1024, 1024], P('blk', None, 'grp'), may hold values from -0.1875 to 0.1875
- neighbour_mask: int32 [128, 4], P('blk'), may hold values 0 or 1
- sketch: float32 [5, 256, 32], replicated, may hold values from -6 to 6
Outputs:
- bases: float32 [128, 1024, 32], P('blk', 'grp')
- reduced_coupling: float32 [128, 4, 32, 32], P('blk')
- reduced_excitation: float32 [128, 32, 256], P('blk')
The draws below stay inside these ranges and needn't reach their ends.
Inputs may be any that keep to these rules, and one draw needn't show every extreme that they name: `neighbour_mask`: 1 where the block at that slot's offset adds secondary currents, 0 where it does not; slots pointing outside the array add nothing in any case.
All inputs are finite; a program needn't handle non-finite values.
Results may differ from the reference program's by a relative error of at most 0.0003.
Values sent between devices are 32-bit elements; how exact they have to be, the bound alone decides.
No kernel may reach another device: no remote copies, remote signals or barrier semaphores. Data moves between devices by JAX's collectives and lax.ppermute only.
A program may use at most 64 MiB of HBM per device.

```python
import math
import jax
import jax.numpy as jnp
from jax import lax

N = 1024
P_SIZE = 256
R = 32
K = 4
NB = 128


def set_ends(entries, rng, least, top_value):
    longest = entries.shape.index(max(entries.shape))
    spots = []
    for shift in (0, 1):
        where = [jax.random.randint(jax.random.fold_in(rng, axis), (), 0, length) for axis, length in enumerate(entries.shape)]
        where[longest] = (where[longest] + shift) % entries.shape[longest]
        spots.append(tuple(where))
    return entries.at[spots[0]].set(least).at[spots[1]].set(top_value)


def level_of(stream_key, dims, pieces, low, high):
    factor_of, own = 1.0, jax.random.fold_in(stream_key, 6)
    for axis_at, shards_of in pieces:
        steps = jnp.exp(jax.random.uniform(jax.random.fold_in(own, axis_at), (shards_of,), jnp.float32, low / len(pieces), high / len(pieces)))
        factor_of = factor_of * jnp.repeat(steps, dims[axis_at] // shards_of).reshape([-1 if axis == axis_at else 1 for axis in range(len(dims))])
    return factor_of


def gaussian(key, extent, width, bound, cuts=(), kind=jnp.bfloat16):
    drawn = width * jax.random.normal(key, extent, jnp.float32)
    if cuts:
        drawn = drawn * level_of(key, extent, cuts, -0.22, 0.18)
    return jnp.clip(drawn, -bound, bound).astype(kind)


def setup_inputs(seed: int = 0) -> dict:
    key_of = jax.random.split(jax.random.key(seed), 6)
    return {
        "excitation": gaussian(key_of[0], (NB, N, P_SIZE), 1.0, 6.0, ((0, 64),)),
        "inverse_self": gaussian(key_of[1], (NB, N, N), N ** -0.5, 0.1875, ((0, 64), (1, 8))),
        "coupling": gaussian(key_of[2], (NB, K, N, N), N ** -0.5, 0.1875, ((0, 64), (2, 8))),
        "neighbour_mask": set_ends((jax.random.randint(key_of[3], (NB, K), 0, 4) < 3).astype(jnp.int32), jax.random.fold_in(key_of[3], 1), 0, 1),
        "sketch": gaussian(key_of[4], (K + 1, P_SIZE, R), 1.0, 6.0, (), jnp.float32),
    }


neighbour_offsets = (-2, -1, 1, 2)

def exact_dot(left, right):
    return jnp.dot(left.astype(jnp.float32), right.astype(jnp.float32), precision=lax.Precision.HIGHEST, preferred_element_type=jnp.float32)

def reference(excitation, inverse_self, coupling, neighbour_mask, sketch):
    primary = lax.map(lambda pair: jnp.dot(pair[0].astype(jnp.float32), pair[1].astype(jnp.float32), preferred_element_type=jnp.float32), (inverse_self, excitation))
    padding = jnp.zeros((2, N, P_SIZE), jnp.float32)
    padded = jnp.concatenate([padding, primary, padding], axis=0)
    weights_mask = neighbour_mask.astype(jnp.float32)

    def sketch_block(index):
        beside_all = lax.dynamic_slice_in_dim(padded, index, 5, 0)
        sources = jnp.zeros((N, R), jnp.float32)
        for slot_index, offset in enumerate(neighbour_offsets):
            coupled = exact_dot(coupling[index, slot_index], beside_all[2 + offset])
            coupled = exact_dot(coupled, sketch[slot_index + 1])
            sources = sources + weights_mask[index, slot_index] * coupled
        own_part = exact_dot(primary[index], sketch[0])
        return own_part - exact_dot(inverse_self[index], sources)
    sketched = lax.map(sketch_block, jnp.arange(NB, dtype=jnp.int32))
    gram = jnp.einsum('bnr,bns->brs', sketched, sketched, precision=lax.Precision.HIGHEST) / N
    chol_lower = jnp.linalg.cholesky(gram)
    bases = lax.linalg.triangular_solve(chol_lower, sketched, left_side=False, lower=True, transpose_a=True)
    base_pad = jnp.zeros((2, N, R), jnp.float32)
    padded_bases = jnp.concatenate([base_pad, bases, base_pad], axis=0)
    norm_scale = 1.0 / math.sqrt(N)

    def reduce_block(index):
        beside_all = lax.dynamic_slice_in_dim(padded_bases, index, 5, 0)
        own_basis = bases[index]
        stacked = []
        for slot_index, offset in enumerate(neighbour_offsets):
            coupled = exact_dot(coupling[index, slot_index], beside_all[2 + offset])
            stacked.append(exact_dot(own_basis.T, coupled))
        driven = exact_dot(own_basis.T, excitation[index])
        return (jnp.stack(stacked, axis=0) * norm_scale, driven * norm_scale)
    reduced_coupling, reduced_excitation = lax.map(reduce_block, jnp.arange(NB, dtype=jnp.int32))
    return (bases, reduced_coupling, reduced_excitation)
```

```python
import functools

import jax
import jax.numpy as jnp
from jax import lax
from jax.experimental import pallas as pl
from jax.experimental.pallas import tpu as pltpu
from jax.sharding import PartitionSpec as P

F32, BF16 = jnp.float32, jnp.bfloat16
NT = (((1,), (1,)), ((), ()))
NN = (((1,), (0,)), ((), ()))
chip_groups = [[0, 2, 4, 6], [1, 3, 5, 7]]
core_groups = [[0, 1], [2, 3], [4, 5], [6, 7]]


def halves(value):
    high = value.astype(BF16)
    return high, (value - high.astype(F32)).astype(BF16)


def stacked_halves(value):
    return jnp.concatenate(halves(value), axis=0)


def dot(left, right, dims):
    return lax.dot_general(left, right, dims, preferred_element_type=F32)


def folded(left, right, dims):
    rows = left.shape[0]
    both = dot(stacked_halves(left), right, dims)
    return both[:rows] + both[rows:]


def exact(left, right, dims):
    rows = left.shape[0]
    right_high, right_low = halves(right)
    left_high, left_low = halves(left)
    both = dot(jnp.concatenate([left_high, left_low], axis=0), right_high, dims)
    return both[:rows] + (both[rows:] + dot(left_high, right_low, dims))


def call(kernel, outs, *, scratch=(), smem=0, vmem=32):
    def run(*args):
        specs = [pl.BlockSpec(memory_space=pltpu.SMEM)] * smem
        specs += [pl.BlockSpec(memory_space=pltpu.VMEM)] * (len(args) - smem)
        return pl.pallas_call(
            kernel,
            out_shape=[jax.ShapeDtypeStruct(shape, F32) for shape in outs],
            in_specs=specs,
            out_specs=[pl.BlockSpec(memory_space=pltpu.VMEM)] * len(outs),
            scratch_shapes=list(scratch),
            compiler_params=pltpu.CompilerParams(vmem_limit_bytes=vmem << 20),
        )(*args)

    return run


def primary_kernel(place, exc, inv, sk, own, local, first, second):
    parity = place[0]
    rows = []
    for i in range(2):
        primary = dot(inv[i], exc[i], NN)
        rows.append(exact(sk[...], primary, NT))
        own[i] = rows[i][0:32]
    part = lambda i, k: rows[i][32 * k : 32 * k + 32]
    local[0] = part(1, 3)
    local[1] = part(0, 2)
    up = [part(0, 1), part(1, 1), part(1, 2)]
    down = [part(0, 4), part(1, 4), part(0, 3)]
    even = parity == 0
    for n in range(3):
        first[n] = jnp.where(even, up[n], down[n])
        second[n] = jnp.where(even, down[n], up[n])


def sources_kernel(place, mask, same, other, coup, out, high, low):
    parity, core = place[0], place[1]
    for z in range(4):
        for piece in range(8):
            for src, c in ((same, core), (other, 1 - core)):
                h, l = halves(src[z, piece])
                high[2 * z + c, piece] = h
                low[2 * z + c, piece] = l

    def piece_of(n):
        return jnp.concatenate(
            [
                jnp.concatenate([high[g, n] for g in range(8)], axis=1),
                jnp.concatenate([low[g, n] for g in range(8)], axis=1),
            ],
            axis=0,
        )

    before = 5 - 3 * parity
    after = 2 + 3 * parity
    table = (
        (before, before + 2, 0, after),
        (before + 1, 1, after + 2, after + 1),
    )
    for i in range(2):
        total = jnp.zeros((32, 128), F32)
        for k in range(4):
            both = dot(piece_of(table[i][k]), coup[i, k], NT)
            total = total + mask[i, k].astype(F32) * (both[:32] + both[32:])
        for z in range(4):
            out[z, i] = total


def sketched_kernel(own, src, inv, out):
    for i in range(2):
        whole = jnp.concatenate([src[g % 2, g // 2, i] for g in range(8)], axis=1)
        out[i] = own[i] - folded(whole, inv[i], NT)


def lower_inverse(gram):
    n = gram.shape[0]
    row = lax.broadcasted_iota(jnp.int32, (n, 32, 32), 1)
    col = lax.broadcasted_iota(jnp.int32, (n, 32, 32), 2)
    inverse = jnp.where(row == col, 1.0, 0.0).astype(F32)
    work = gram
    for j in range(32):
        scale = lax.rsqrt(work[:, j : j + 1, j : j + 1])
        pivot = work[:, j : j + 1, :] * scale
        pivot_inverse = inverse[:, j : j + 1, :] * scale
        factor = work[:, :, j : j + 1] * scale
        below = jnp.where(row[:, :, 0:1] > j, factor, 0.0)
        at = row == j
        inverse = jnp.where(at, pivot_inverse, inverse - below * pivot_inverse)
        work = work - below * pivot
    return inverse


def reduce_kernel(place, near, mine, exc, coup, bases, coupled, driven):
    parity = place[0]
    whole = []
    grams = []
    for n in range(6):
        w = jnp.concatenate([near[g, n] for g in range(8)], axis=1)
        whole.append(w)
        grams.append(
            lax.dot_general(
                w, w, NT, precision=lax.Precision.HIGHEST, preferred_element_type=F32
            )
            * (1.0 / 1024)
        )
    diagonal = lax.broadcasted_iota(jnp.int32, (32, 32), 0) == lax.broadcasted_iota(
        jnp.int32, (32, 32), 1
    )
    absent = jnp.where(diagonal, 1.0 - place[2].astype(F32), 0.0)
    grams[4] = grams[4] + absent
    grams[5] = grams[5] + absent
    inverse = lower_inverse(jnp.stack(grams))
    full = [exact(inverse[n], whole[n], NN) for n in range(6)]
    even = parity == 0
    before = [jnp.where(even, full[4 + n], full[2 + n]) for n in range(2)]
    after = [jnp.where(even, full[2 + n], full[4 + n]) for n in range(2)]
    line = [before[0], before[1], full[0], full[1], after[0], after[1]]
    for i in range(2):
        part = exact(inverse[i], mine[i], NN)
        bases[i] = part.T
        driven[i] = folded(full[i], exc[i], NN) * (1.0 / 32)
        stack = []
        for k, o in enumerate((-2, -1, 1, 2)):
            stack.append(folded(line[2 + i + o], coup[i, k], NT))
        value = exact(part, jnp.concatenate(stack, axis=0), NT) * (1.0 / 32)
        for z in range(4):
            coupled[z, i] = value


def sum_kernel(parts, out):
    total = parts[0, 0]
    for g in range(1, 8):
        total = total + parts[g % 2, g // 2]
    for i in range(2):
        for k in range(4):
            out[i, k] = total[i, :, 32 * k : 32 * k + 32]


def exchange(first, second):
    size = lax.axis_size("blk")

    def pairs(start):
        ups = [(i, i + 1) for i in range(start, size - 1, 2)]
        return ups + [(j, i) for i, j in ups]

    got_second = lax.ppermute(second, "blk", pairs(1))
    got_first = lax.ppermute(first, "blk", pairs(0))
    return got_first, got_second


def share(value):
    over_chips = lax.all_to_all(value, "grp", 0, 0, axis_index_groups=chip_groups)
    return lax.all_gather(over_chips, "grp", axis=0, axis_index_groups=core_groups)


def shards(excitation, inverse_self, coupling, neighbour_mask, sketch):
    block_at, member = lax.axis_index("blk"), lax.axis_index("grp")
    inner = (block_at > 0) & (block_at < lax.axis_size("blk") - 1)
    place = jnp.stack([block_at % 2, member % 2, inner.astype(jnp.int32)])
    turned = sketch.transpose(0, 2, 1).reshape(160, 256)
    own, local, first, second = call(
        primary_kernel, [(2, 32, 128), (2, 32, 128), (3, 32, 128), (3, 32, 128)], smem=1
    )(place, excitation, inverse_self, turned)
    got_first, got_second = exchange(first, second)
    pieces = jnp.concatenate([local, got_first, got_second], axis=0)
    same = lax.all_gather(pieces, "grp", axis=0, axis_index_groups=chip_groups)
    other = lax.ppermute(same, "grp", [(g, g ^ 1) for g in range(8)])
    (sources,) = call(
        sources_kernel,
        [(4, 2, 32, 128)],
        smem=2,
        scratch=[pltpu.VMEM((8, 8, 32, 128), BF16), pltpu.VMEM((8, 8, 32, 128), BF16)],
    )(place, neighbour_mask, same, other, coupling)
    (sketched,) = call(sketched_kernel, [(2, 32, 128)])(own, share(sources), inverse_self)
    got_first, got_second = exchange(sketched, sketched)
    near = lax.all_gather(
        jnp.concatenate([sketched, got_first, got_second], axis=0), "grp", axis=0
    )
    bases, coupled, driven = call(
        reduce_kernel, [(2, 128, 32), (4, 2, 32, 128), (2, 32, 256)], smem=1
    )(place, near, sketched, excitation, coupling)
    (reduced,) = call(sum_kernel, [(2, 4, 32, 32)])(share(coupled))
    return bases, reduced, driven


def solution(mesh):
    return jax.shard_map(
        shards,
        mesh=mesh,
        in_specs=(
            P("blk", None, None),
            P("blk", "grp", None),
            P("blk", None, "grp", None),
            P("blk", None),
            P(),
        ),
        out_specs=(P("blk", "grp", None), P("blk", None, None, None), P("blk", None, None)),
        check_vma=False,
    )
```

```python
import jax
import jax.numpy as jnp
from jax import lax
from jax.experimental import pallas as pl
from jax.experimental.pallas import tpu as pltpu
from jax.sharding import PartitionSpec as P


F32, BF16 = jnp.float32, jnp.bfloat16
NT = (((1,), (1,)), ((), ()))
NN = (((1,), (0,)), ((), ()))
chip_groups = [[0, 2, 4, 6], [1, 3, 5, 7]]
core_groups = [[0, 1], [2, 3], [4, 5], [6, 7]]


def halves(value):
    high = value.astype(BF16)
    return high, (value - high.astype(F32)).astype(BF16)


def stacked_halves(value):
    return jnp.concatenate(halves(value), axis=0)


def dot(left, right, dims):
    return lax.dot_general(left, right, dims, preferred_element_type=F32)


def folded(left, right, dims):
    rows = left.shape[0]
    both = dot(stacked_halves(left), right, dims)
    return both[:rows] + both[rows:]


def exact(left, right, dims):
    rows = left.shape[0]
    right_high, right_low = halves(right)
    left_high, left_low = halves(left)
    both = dot(jnp.concatenate([left_high, left_low], axis=0), right_high, dims)
    return both[:rows] + (both[rows:] + dot(left_high, right_low, dims))


def call(kernel, outs, *, scratch=(), smem=0, hbm=0, vmem=32):
    def run(*args):
        specs = [pl.BlockSpec(memory_space=pltpu.SMEM)] * smem
        specs += [pl.BlockSpec(memory_space=pltpu.HBM)] * hbm
        specs += [pl.BlockSpec(memory_space=pltpu.VMEM)] * (len(args) - smem - hbm)
        return pl.pallas_call(
            kernel,
            out_shape=[jax.ShapeDtypeStruct(shape, F32) for shape in outs],
            in_specs=specs,
            out_specs=[pl.BlockSpec(memory_space=pltpu.VMEM)] * len(outs),
            scratch_shapes=list(scratch),
            compiler_params=pltpu.CompilerParams(vmem_limit_bytes=vmem << 20),
        )(*args)

    return run


def primary_kernel(place, exc_hbm, inv_hbm, sk_hbm, own, local, first, second, exc, inv, sk, sems):
    copies = [pltpu.make_async_copy(sk_hbm, sk, sems.at[0])]
    for i in range(2):
        copies.append(pltpu.make_async_copy(inv_hbm.at[i], inv.at[i], sems.at[1 + i]))
        copies.append(pltpu.make_async_copy(exc_hbm.at[i], exc.at[i], sems.at[3 + i]))
    for copy in copies:
        copy.start()
    parity = place[0]
    rows = []
    for i in range(2):
        copies[1 + 2 * i].wait()
        copies[2 + 2 * i].wait()
        primary = dot(inv[i], exc[i], NN)
        if i == 0:
            copies[0].wait()
        rows.append(exact(sk[...], primary, NT))
        own[i] = rows[i][0:32]
    part = lambda i, k: rows[i][32 * k : 32 * k + 32]
    local[0] = part(1, 3)
    local[1] = part(0, 2)
    up = [part(0, 1), part(1, 1), part(1, 2)]
    down = [part(0, 4), part(1, 4), part(0, 3)]
    even = parity == 0
    for n in range(3):
        first[n] = jnp.where(even, up[n], down[n])
        second[n] = jnp.where(even, down[n], up[n])


def sources_kernel(place, mask, same, other, coup, out, high, low):
    parity, core = place[0], place[1]
    for z in range(4):
        for piece in range(8):
            for src, c in ((same, core), (other, 1 - core)):
                h, l = halves(src[z, piece])
                high[2 * z + c, piece] = h
                low[2 * z + c, piece] = l

    def piece_of(n):
        return jnp.concatenate(
            [
                jnp.concatenate([high[g, n] for g in range(8)], axis=1),
                jnp.concatenate([low[g, n] for g in range(8)], axis=1),
            ],
            axis=0,
        )

    before = 5 - 3 * parity
    after = 2 + 3 * parity
    table = (
        (before, before + 2, 0, after),
        (before + 1, 1, after + 2, after + 1),
    )
    for i in range(2):
        total = jnp.zeros((32, 128), F32)
        for k in range(4):
            both = dot(piece_of(table[i][k]), coup[i, k], NT)
            total = total + mask[i, k].astype(F32) * (both[:32] + both[32:])
        for z in range(4):
            out[z, i] = total


def sketched_kernel(own, src, inv, out):
    for i in range(2):
        whole = jnp.concatenate([src[g % 2, g // 2, i] for g in range(8)], axis=1)
        out[i] = own[i] - folded(whole, inv[i], NT)


def thirds(value):
    high, rest = value.astype(BF16), value
    rest = rest - high.astype(F32)
    middle = rest.astype(BF16)
    return [high, middle, (rest - middle.astype(F32)).astype(BF16)]


def best(left, right, dims):
    return lax.dot_general(
        left, right, dims, precision=lax.Precision.HIGHEST, preferred_element_type=F32
    )


def lanes(near, n):
    return jnp.concatenate([near[g, n] for g in range(8)], axis=1)


def products_kernel(place, near, mine, coup, out):
    even = place[0] == 0
    own = [lanes(near, 0), lanes(near, 1)]
    first = [lanes(near, 2), lanes(near, 3)]
    second = [lanes(near, 4), lanes(near, 5)]
    before = [jnp.where(even, second[n], first[n]) for n in range(2)]
    after = [jnp.where(even, first[n], second[n]) for n in range(2)]
    line = [jnp.concatenate(thirds(w), axis=0) for w in before + own + after]
    for i in range(2):
        stack = []
        for k, o in enumerate((-2, -1, 1, 2)):
            both = dot(line[2 + i + o], coup[i, k], NT)
            stack.append(both[:32] + (both[32:64] + both[64:]))
        value = best(mine[i], jnp.concatenate(stack, axis=0), NT)
        for z in range(4):
            out[z, i] = value


def lower_inverse(gram):
    n = gram.shape[0]
    row = lax.broadcasted_iota(jnp.int32, (n, 32, 32), 1)
    col = lax.broadcasted_iota(jnp.int32, (n, 32, 32), 2)
    work = jnp.concatenate([gram, jnp.where(row == col, 1.0, 0.0).astype(F32)], axis=2)
    tiles = [work[:, 8 * t : 8 * t + 8] for t in range(4)]
    within = lax.broadcasted_iota(jnp.int32, (n, 8, 1), 1)
    for j in range(32):
        at, r = divmod(j, 8)
        pivot = tiles[at][:, r : r + 1, :]
        pivot = pivot * (1.0 / pivot[:, :, j : j + 1])
        for t in range(at, 4):
            factor = tiles[t][:, :, j : j + 1]
            if t == at:
                factor = jnp.where(within > r, factor, 0.0)
            tiles[t] = tiles[t] - factor * pivot
    work = jnp.concatenate(tiles, axis=1)
    diagonal = jnp.sum(jnp.where(row == col, work[:, :, :32], 0.0), axis=2, keepdims=True)
    return work[:, :, 32:] * lax.rsqrt(diagonal)


def factor_kernel(place, exc_hbm, near, mine, bases, driven, left, right, exc, sem):
    copy = pltpu.make_async_copy(exc_hbm, exc, sem)
    copy.start()
    even = place[0] == 0
    whole = [lanes(near, n) for n in range(6)]
    grams = [best(w, w, NT) * (1.0 / 1024) for w in whole]
    diagonal = lax.broadcasted_iota(jnp.int32, (32, 32), 0) == lax.broadcasted_iota(
        jnp.int32, (32, 32), 1
    )
    absent = jnp.where(diagonal, 1.0 - place[2].astype(F32), 0.0)
    grams[4] = grams[4] + absent
    grams[5] = grams[5] + absent
    inverse = lower_inverse(jnp.stack(grams))
    before = [jnp.where(even, inverse[4 + n], inverse[2 + n]) for n in range(2)]
    after = [jnp.where(even, inverse[2 + n], inverse[4 + n]) for n in range(2)]
    line = before + [inverse[0], inverse[1]] + after
    right[...] = jnp.zeros((2, 128, 128), F32)
    copy.wait()
    for i in range(2):
        bases[i] = exact(inverse[i], mine[i], NN)
        full = exact(inverse[i], whole[i], NN)
        driven[i] = folded(full, exc[i], NN) * (1.0 / 32)
        left[i] = inverse[i] * (1.0 / 32)
        for k, o in enumerate((-2, -1, 1, 2)):
            at = slice(32 * k, 32 * k + 32)
            right[i, at, at] = line[2 + i + o]


def sum_kernel(parts, left, right, out):
    total = parts[0, 0]
    for g in range(1, 8):
        total = total + parts[g % 2, g // 2]
    for i in range(2):
        value = best(best(left[i], total[i], NN), right[i], NT)
        for k in range(4):
            out[i, k] = value[:, 32 * k : 32 * k + 32]


def in_hbm(value):
    return pltpu.with_memory_space_constraint(value, pltpu.HBM)


def exchange(first, second):
    size = lax.axis_size("blk")

    def pairs(start):
        ups = [(i, i + 1) for i in range(start, size - 1, 2)]
        return ups + [(j, i) for i, j in ups]

    got_second = lax.ppermute(second, "blk", pairs(1))
    got_first = lax.ppermute(first, "blk", pairs(0))
    return got_first, got_second


def over_chips(value):
    return lax.all_to_all(value, "grp", 0, 0, axis_index_groups=chip_groups)


def over_cores(value):
    return lax.all_gather(value, "grp", axis=0, axis_index_groups=core_groups)


def shards(excitation, inverse_self, coupling, neighbour_mask, sketch):
    block_at = lax.axis_index("blk")
    inner = (block_at > 0) & (block_at < lax.axis_size("blk") - 1)
    place = jnp.stack([block_at % 2, lax.axis_index("grp") % 2, inner.astype(jnp.int32)])
    turned = sketch.transpose(0, 2, 1).reshape(160, 256)
    own, local, first, second = call(
        primary_kernel,
        [(2, 32, 128), (2, 32, 128), (3, 32, 128), (3, 32, 128)],
        smem=1,
        hbm=3,
        scratch=[
            pltpu.VMEM((2, 1024, 256), BF16),
            pltpu.VMEM((2, 128, 1024), BF16),
            pltpu.VMEM((160, 256), F32),
            pltpu.SemaphoreType.DMA((5,)),
        ],
    )(place, in_hbm(excitation), in_hbm(inverse_self), in_hbm(turned))
    got_first, got_second = exchange(first, second)
    pieces = jnp.concatenate([local, got_first, got_second], axis=0)
    same = lax.all_gather(pieces, "grp", axis=0, axis_index_groups=chip_groups)
    other = lax.ppermute(same, "grp", [(g, g ^ 1) for g in range(8)])
    (sources,) = call(
        sources_kernel,
        [(4, 2, 32, 128)],
        smem=2,
        scratch=[pltpu.VMEM((8, 8, 32, 128), BF16), pltpu.VMEM((8, 8, 32, 128), BF16)],
    )(place, neighbour_mask, same, other, coupling)
    whole_sources = over_cores(over_chips(sources))
    (sketched,) = call(sketched_kernel, [(2, 32, 128)])(own, whole_sources, inverse_self)
    got_first, got_second = exchange(sketched, sketched)
    near = lax.all_gather(
        jnp.concatenate([sketched, got_first, got_second], axis=0), "grp", axis=0
    )
    (products,) = call(products_kernel, [(4, 2, 32, 128)], smem=1)(
        place, near, sketched, coupling
    )
    parts = over_chips(products)
    bases, driven, left, right = call(
        factor_kernel,
        [(2, 32, 128), (2, 32, 256), (2, 32, 32), (2, 128, 128)],
        smem=1,
        hbm=1,
        scratch=[pltpu.VMEM((2, 1024, 256), BF16), pltpu.SemaphoreType.DMA],
    )(place, in_hbm(excitation), near, sketched)
    (reduced,) = call(sum_kernel, [(2, 4, 32, 32)])(over_cores(parts), left, right)
    return bases.transpose(0, 2, 1), reduced, driven


def solution(mesh):
    return jax.shard_map(
        shards,
        mesh=mesh,
        in_specs=(
            P("blk", None, None),
            P("blk", "grp", None),
            P("blk", None, "grp", None),
            P("blk", None),
            P(),
        ),
        out_specs=(P("blk", "grp", None), P("blk", None, None, None), P("blk", None, None)),
        check_vma=False,
    )
```

```python
import jax
import jax.numpy as jnp
from jax import lax
from jax.experimental import pallas as pl
from jax.experimental.pallas import tpu as pltpu
from jax.sharding import PartitionSpec as P


F32, BF16 = jnp.float32, jnp.bfloat16
NT = (((1,), (1,)), ((), ()))
NN = (((1,), (0,)), ((), ()))
chip_groups = [[0, 2, 4, 6], [1, 3, 5, 7]]
core_groups = [[0, 1], [2, 3], [4, 5], [6, 7]]
run_length = 8


def halves(value):
    high = value.astype(BF16)
    return high, (value - high.astype(F32)).astype(BF16)


def stacked_halves(value):
    return jnp.concatenate(halves(value), axis=0)


def dot(left, right, dims):
    return lax.dot_general(left, right, dims, preferred_element_type=F32)


def folded(left, right, dims):
    rows = left.shape[0]
    both = dot(stacked_halves(left), right, dims)
    return both[:rows] + both[rows:]


def exact(left, right, dims):
    rows = left.shape[0]
    right_high, right_low = halves(right)
    left_high, left_low = halves(left)
    both = dot(jnp.concatenate([left_high, left_low], axis=0), right_high, dims)
    return both[:rows] + (both[rows:] + dot(left_high, right_low, dims))


def call(kernel, outs, *, scratch=(), smem=0, hbm=0, vmem=32):
    def run(*args):
        specs = [pl.BlockSpec(memory_space=pltpu.SMEM)] * smem
        specs += [pl.BlockSpec(memory_space=pltpu.HBM)] * hbm
        specs += [pl.BlockSpec(memory_space=pltpu.VMEM)] * (len(args) - smem - hbm)
        return pl.pallas_call(
            kernel,
            out_shape=[jax.ShapeDtypeStruct(shape, F32) for shape in outs],
            in_specs=specs,
            out_specs=[pl.BlockSpec(memory_space=pltpu.VMEM)] * len(outs),
            scratch_shapes=list(scratch),
            compiler_params=pltpu.CompilerParams(vmem_limit_bytes=vmem << 20),
        )(*args)

    return run


def primary_kernel(place, exc_hbm, inv_hbm, sk_hbm, own, local, first, second, exc, inv, sk, sems):
    copies = [pltpu.make_async_copy(sk_hbm, sk, sems.at[0])]
    for i in range(2):
        copies.append(pltpu.make_async_copy(inv_hbm.at[i], inv.at[i], sems.at[1 + i]))
        copies.append(pltpu.make_async_copy(exc_hbm.at[i], exc.at[i], sems.at[3 + i]))
    for copy in copies:
        copy.start()
    parity = place[0]
    rows = []
    for i in range(2):
        copies[1 + 2 * i].wait()
        copies[2 + 2 * i].wait()
        primary = dot(inv[i], exc[i], NN)
        if i == 0:
            copies[0].wait()
        rows.append(exact(sk[...], primary, NT))
        own[i] = rows[i][0:32]
    part = lambda i, k: rows[i][32 * k : 32 * k + 32]
    local[0] = part(1, 3)
    local[1] = part(0, 2)
    up = [part(0, 1), part(1, 1), part(1, 2)]
    down = [part(0, 4), part(1, 4), part(0, 3)]
    even = parity == 0
    for n in range(3):
        first[n] = jnp.where(even, up[n], down[n])
        second[n] = jnp.where(even, down[n], up[n])


def sources_kernel(place, mask, same, other, coup, out, high, low):
    parity, core, turn = place[0], place[1], place[3]
    for z in range(4):
        for piece in range(8):
            for src, c in ((same, core), (other, 1 - core)):
                g = 2 * z + c
                if piece >= 5:
                    g = (g + 4 * turn) & 7
                high[g, piece], low[g, piece] = halves(src[z, piece])

    def piece_of(n):
        return jnp.concatenate(
            [
                jnp.concatenate([high[g, n] for g in range(8)], axis=1),
                jnp.concatenate([low[g, n] for g in range(8)], axis=1),
            ],
            axis=0,
        )

    before = 5 - 3 * parity
    after = 2 + 3 * parity
    table = (
        (before, before + 2, 0, after),
        (before + 1, 1, after + 2, after + 1),
    )
    for i in range(2):
        total = jnp.zeros((32, 128), F32)
        for k in range(4):
            both = dot(piece_of(table[i][k]), coup[i, k], NT)
            total = total + mask[i, k].astype(F32) * (both[:32] + both[32:])
        for z in range(4):
            out[z, i] = total


def sketched_kernel(own, src, inv, out):
    for i in range(2):
        whole = jnp.concatenate([src[g % 2, g // 2, i] for g in range(8)], axis=1)
        out[i] = own[i] - folded(whole, inv[i], NT)


def thirds(value):
    high, rest = value.astype(BF16), value
    rest = rest - high.astype(F32)
    middle = rest.astype(BF16)
    return [high, middle, (rest - middle.astype(F32)).astype(BF16)]


def best(left, right, dims):
    return lax.dot_general(
        left, right, dims, precision=lax.Precision.HIGHEST, preferred_element_type=F32
    )


def lanes(near, n, turn=None):
    at = range(8) if turn is None else [(g + 4 * turn) & 7 for g in range(8)]
    return jnp.concatenate([near[g, n] for g in at], axis=1)


def products_kernel(place, near, mine, coup, out):
    even = place[0] == 0
    own = [lanes(near, 0), lanes(near, 1)]
    first = [lanes(near, 2), lanes(near, 3)]
    second = [lanes(near, 4, place[3]), lanes(near, 5, place[3])]
    before = [jnp.where(even, second[n], first[n]) for n in range(2)]
    after = [jnp.where(even, first[n], second[n]) for n in range(2)]
    line = [jnp.concatenate(thirds(w), axis=0) for w in before + own + after]
    for i in range(2):
        stack = []
        for k, o in enumerate((-2, -1, 1, 2)):
            both = dot(line[2 + i + o], coup[i, k], NT)
            stack.append(both[:32] + (both[32:64] + both[64:]))
        value = best(mine[i], jnp.concatenate(stack, axis=0), NT)
        for z in range(4):
            out[z, i] = value


def lower_inverse(gram):
    n = gram.shape[0]
    row = lax.broadcasted_iota(jnp.int32, (n, 32, 32), 1)
    col = lax.broadcasted_iota(jnp.int32, (n, 32, 32), 2)
    work = jnp.concatenate([gram, jnp.where(row == col, 1.0, 0.0).astype(F32)], axis=2)
    tiles = [work[:, 8 * t : 8 * t + 8] for t in range(4)]
    within = lax.broadcasted_iota(jnp.int32, (n, 8, 1), 1)
    for j in range(32):
        at, r = divmod(j, 8)
        pivot = tiles[at][:, r : r + 1, :]
        pivot = pivot * (1.0 / pivot[:, :, j : j + 1])
        for t in range(at, 4):
            factor = tiles[t][:, :, j : j + 1]
            if t == at:
                factor = jnp.where(within > r, factor, 0.0)
            tiles[t] = tiles[t] - factor * pivot
    work = jnp.concatenate(tiles, axis=1)
    diagonal = jnp.sum(jnp.where(row == col, work[:, :, :32], 0.0), axis=2, keepdims=True)
    return work[:, :, 32:] * lax.rsqrt(diagonal)


def factor_kernel(place, exc_hbm, near, mine, bases, driven, left, right, exc, sem):
    copy = pltpu.make_async_copy(exc_hbm, exc, sem)
    copy.start()
    even = place[0] == 0
    whole = [lanes(near, n) for n in range(6)]
    grams = [exact(w, w, NT) * (1.0 / 1024) for w in whole]
    diagonal = lax.broadcasted_iota(jnp.int32, (32, 32), 0) == lax.broadcasted_iota(
        jnp.int32, (32, 32), 1
    )
    absent = jnp.where(diagonal, 1.0 - place[2].astype(F32), 0.0)
    grams[4] = grams[4] + absent
    grams[5] = grams[5] + absent
    inverse = lower_inverse(jnp.stack(grams))
    before = [jnp.where(even, inverse[4 + n], inverse[2 + n]) for n in range(2)]
    after = [jnp.where(even, inverse[2 + n], inverse[4 + n]) for n in range(2)]
    line = before + [inverse[0], inverse[1]] + after
    right[...] = jnp.zeros((2, 128, 128), F32)
    copy.wait()
    for i in range(2):
        bases[i] = exact(inverse[i], mine[i], NN)
        full = exact(inverse[i], whole[i], NN)
        driven[i] = folded(full, exc[i], NN) * (1.0 / 32)
        left[i] = inverse[i] * (1.0 / 32)
        for k, o in enumerate((-2, -1, 1, 2)):
            at = slice(32 * k, 32 * k + 32)
            right[i, at, at] = line[2 + i + o]


def sum_kernel(parts, left, right, out):
    total = parts[0, 0]
    for g in range(1, 8):
        total = total + parts[g % 2, g // 2]
    for i in range(2):
        value = best(best(left[i], total[i], NN), right[i], NT)
        for k in range(4):
            out[i, k] = value[:, 32 * k : 32 * k + 32]


def in_hbm(value):
    return pltpu.with_memory_space_constraint(value, pltpu.HBM)


def in_vmem(value):
    return pltpu.with_memory_space_constraint(value, pltpu.VMEM)


def exchange(first, second):
    size, width = lax.axis_size("blk"), lax.axis_size("grp")

    def pairs(start):
        both = []
        for i in range(start, size - 1, 2):
            turn = width // 2 if i % run_length == run_length - 1 else 0
            for g in range(width):
                here, there = i * width + g, (i + 1) * width + (g ^ turn)
                both += [(here, there), (there, here)]
        return both

    axes = ("blk", "grp")
    got_second = lax.ppermute(second, axes, pairs(1))
    got_first = lax.ppermute(first, axes, pairs(0))
    return got_first, got_second


def over_chips(value):
    return lax.all_to_all(value, "grp", 0, 0, axis_index_groups=chip_groups)


def over_cores(value):
    return lax.all_gather(value, "grp", axis=0, axis_index_groups=core_groups)


def shards(excitation, inverse_self, coupling, neighbour_mask, sketch):
    block_at = lax.axis_index("blk")
    inner = (block_at > 0) & (block_at < lax.axis_size("blk") - 1)
    turned = ((block_at + 1) % run_length) < 2
    place = jnp.stack(
        [block_at % 2, lax.axis_index("grp") % 2, inner.astype(jnp.int32), turned.astype(jnp.int32)]
    )
    tests = sketch.transpose(0, 2, 1).reshape(160, 256)
    own, local, first, second = call(
        primary_kernel,
        [(2, 32, 128), (2, 32, 128), (3, 32, 128), (3, 32, 128)],
        smem=1,
        hbm=3,
        scratch=[
            pltpu.VMEM((2, 1024, 256), BF16),
            pltpu.VMEM((2, 128, 1024), BF16),
            pltpu.VMEM((160, 256), F32),
            pltpu.SemaphoreType.DMA((5,)),
        ],
    )(place, in_hbm(excitation), in_hbm(inverse_self), in_hbm(tests))
    got_first, got_second = exchange(first, second)
    pieces = jnp.concatenate([local, got_first, got_second], axis=0)
    same = lax.all_gather(pieces, "grp", axis=0, axis_index_groups=chip_groups)
    other = lax.ppermute(same, "grp", [(g, g ^ 1) for g in range(8)])
    (sources,) = call(
        sources_kernel,
        [(4, 2, 32, 128)],
        smem=2,
        scratch=[pltpu.VMEM((8, 8, 32, 128), BF16), pltpu.VMEM((8, 8, 32, 128), BF16)],
    )(place, neighbour_mask, same, other, coupling)
    whole_sources = over_cores(over_chips(sources))
    (sketched,) = call(sketched_kernel, [(2, 32, 128)])(own, whole_sources, inverse_self)
    got_first, got_second = exchange(sketched, sketched)
    near = lax.all_gather(
        jnp.concatenate([sketched, got_first, got_second], axis=0), "grp", axis=0
    )
    (products,) = call(products_kernel, [(4, 2, 32, 128)], smem=1)(
        place, near, sketched, coupling
    )
    parts = over_chips(in_vmem(products))
    bases, driven, left, right = call(
        factor_kernel,
        [(2, 32, 128), (2, 32, 256), (2, 32, 32), (2, 128, 128)],
        smem=1,
        hbm=1,
        scratch=[pltpu.VMEM((2, 1024, 256), BF16), pltpu.SemaphoreType.DMA],
    )(place, in_hbm(excitation), near, sketched)
    (reduced,) = call(sum_kernel, [(2, 4, 32, 32)])(over_cores(parts), in_vmem(left), in_vmem(right))
    return bases.transpose(0, 2, 1), reduced, driven


def solution(mesh):
    return jax.shard_map(
        shards,
        mesh=mesh,
        in_specs=(
            P("blk", None, None),
            P("blk", "grp", None),
            P("blk", None, "grp", None),
            P("blk", None),
            P(),
        ),
        out_specs=(P("blk", "grp", None), P("blk", None, None, None), P("blk", None, None)),
        check_vma=False,
    )
```

```python
import jax
import jax.numpy as jnp
from jax import lax
from jax.experimental import pallas as pl
from jax.experimental.pallas import tpu as pltpu
from jax.sharding import PartitionSpec as P


F32, BF16 = jnp.float32, jnp.bfloat16
NT = (((1,), (1,)), ((), ()))
NN = (((1,), (0,)), ((), ()))
chip_groups = [[0, 2, 4, 6], [1, 3, 5, 7]]
core_groups = [[0, 1], [2, 3], [4, 5], [6, 7]]
run_length = 8


def halves(value):
    high = value.astype(BF16)
    return high, (value - high.astype(F32)).astype(BF16)


def stacked_halves(value):
    return jnp.concatenate(halves(value), axis=0)


def dot(left, right, dims):
    return lax.dot_general(left, right, dims, preferred_element_type=F32)


def folded(left, right, dims):
    rows = left.shape[0]
    both = dot(stacked_halves(left), right, dims)
    return both[:rows] + both[rows:]


def exact(left, right, dims):
    rows = left.shape[0]
    right_high, right_low = halves(right)
    left_high, left_low = halves(left)
    both = dot(jnp.concatenate([left_high, left_low], axis=0), right_high, dims)
    return both[:rows] + (both[rows:] + dot(left_high, right_low, dims))


def call(kernel, outs, *, scratch=(), hbm=0, vmem=32):
    def run(*args):
        specs = [pl.BlockSpec(memory_space=pltpu.HBM)] * hbm
        specs += [pl.BlockSpec(memory_space=pltpu.VMEM)] * (len(args) - hbm)
        return pl.pallas_call(
            kernel,
            out_shape=[jax.ShapeDtypeStruct(shape, F32) for shape in outs],
            in_specs=specs,
            out_specs=[pl.BlockSpec(memory_space=pltpu.VMEM)] * len(outs),
            scratch_shapes=list(scratch),
            compiler_params=pltpu.CompilerParams(vmem_limit_bytes=vmem << 20),
        )(*args)

    return run


def parity_of():
    return lax.axis_index("blk") % 2


def turn_of():
    return (((lax.axis_index("blk") + 1) & (run_length - 1)) < 2).astype(jnp.int32)


def primary_kernel(exc_hbm, inv_hbm, sk_hbm, own, local, first, second, exc, inv, sk, sems):
    copies = [pltpu.make_async_copy(sk_hbm, sk, sems.at[0])]
    for i in range(2):
        copies.append(pltpu.make_async_copy(inv_hbm.at[i], inv.at[i], sems.at[1 + i]))
        copies.append(pltpu.make_async_copy(exc_hbm.at[i], exc.at[i], sems.at[3 + i]))
    for n in (1, 2, 0, 3, 4):
        copies[n].start()
    parity = parity_of()
    rows = []
    for i in range(2):
        copies[1 + 2 * i].wait()
        copies[2 + 2 * i].wait()
        primary = dot(inv[i], exc[i], NN)
        if i == 0:
            copies[0].wait()
        rows.append(exact(sk[...], primary, NT))
        own[i] = rows[i][0:32]
    part = lambda i, k: rows[i][32 * k : 32 * k + 32]
    local[0] = part(1, 3)
    local[1] = part(0, 2)
    up = [part(0, 1), part(1, 1), part(1, 2)]
    down = [part(0, 4), part(1, 4), part(0, 3)]
    even = parity == 0
    for n in range(3):
        first[n] = jnp.where(even, up[n], down[n])
        second[n] = jnp.where(even, down[n], up[n])


def sources_kernel(mask, same, other, coup, out, high, low):
    parity, core, turn = parity_of(), lax.axis_index("grp") % 2, turn_of()
    for z in range(4):
        for piece in range(8):
            for src, c in ((same, core), (other, 1 - core)):
                g = 2 * z + c
                if piece >= 5:
                    g = (g + 4 * turn) & 7
                high[g, piece], low[g, piece] = halves(src[z, piece])

    def piece_of(n):
        return jnp.concatenate(
            [
                jnp.concatenate([high[g, n] for g in range(8)], axis=1),
                jnp.concatenate([low[g, n] for g in range(8)], axis=1),
            ],
            axis=0,
        )

    before = 5 - 3 * parity
    after = 2 + 3 * parity
    table = (
        (before, before + 2, 0, after),
        (before + 1, 1, after + 2, after + 1),
    )
    weights = mask[...].astype(F32)
    for i in range(2):
        total = jnp.zeros((32, 128), F32)
        for k in range(4):
            both = dot(piece_of(table[i][k]), coup[i, k], NT)
            total = total + weights[i : i + 1, k : k + 1] * (both[:32] + both[32:])
        for z in range(4):
            out[z, i] = total


def sketched_kernel(own, src, inv, out):
    for i in range(2):
        whole = jnp.concatenate([src[g % 2, g // 2, i] for g in range(8)], axis=1)
        out[i] = own[i] - folded(whole, inv[i], NT)


def thirds(value):
    high, rest = value.astype(BF16), value
    rest = rest - high.astype(F32)
    middle = rest.astype(BF16)
    return [high, middle, (rest - middle.astype(F32)).astype(BF16)]


def best(left, right, dims):
    return lax.dot_general(
        left, right, dims, precision=lax.Precision.HIGHEST, preferred_element_type=F32
    )


def lanes(near, n, turn=None):
    at = range(8) if turn is None else [(g + 4 * turn) & 7 for g in range(8)]
    return jnp.concatenate([near[g, n] for g in at], axis=1)


def products_kernel(near, mine, coup, out):
    even = parity_of() == 0
    own = [lanes(near, 0), lanes(near, 1)]
    first = [lanes(near, 2), lanes(near, 3)]
    second = [lanes(near, 4, turn_of()), lanes(near, 5, turn_of())]
    before = [jnp.where(even, second[n], first[n]) for n in range(2)]
    after = [jnp.where(even, first[n], second[n]) for n in range(2)]
    line = [jnp.concatenate(thirds(w), axis=0) for w in before + own + after]
    for i in range(2):
        stack = []
        for k, o in enumerate((-2, -1, 1, 2)):
            both = dot(line[2 + i + o], coup[i, k], NT)
            stack.append(both[:32] + (both[32:64] + both[64:]))
        value = best(mine[i], jnp.concatenate(stack, axis=0), NT)
        for z in range(4):
            out[z, i] = value


def lower_inverse(gram):
    n = gram.shape[0]
    row = lax.broadcasted_iota(jnp.int32, (n, 32, 32), 1)
    col = lax.broadcasted_iota(jnp.int32, (n, 32, 32), 2)
    work = jnp.concatenate([gram, jnp.where(row == col, 1.0, 0.0).astype(F32)], axis=2)
    tiles = [work[:, 8 * t : 8 * t + 8] for t in range(4)]
    within = lax.broadcasted_iota(jnp.int32, (n, 8, 1), 1)
    for j in range(32):
        at, r = divmod(j, 8)
        pivot = tiles[at][:, r : r + 1, :]
        pivot = pivot * (1.0 / pivot[:, :, j : j + 1])
        for t in range(at, 4):
            factor = tiles[t][:, :, j : j + 1]
            if t == at:
                factor = jnp.where(within > r, factor, 0.0)
            tiles[t] = tiles[t] - factor * pivot
    work = jnp.concatenate(tiles, axis=1)
    diagonal = jnp.sum(jnp.where(row == col, work[:, :, :32], 0.0), axis=2, keepdims=True)
    return work[:, :, 32:] * lax.rsqrt(diagonal)


def factor_kernel(exc_hbm, near, mine, bases, driven, left, right, exc, sem):
    copy = pltpu.make_async_copy(exc_hbm, exc, sem)
    copy.start()
    even = parity_of() == 0
    whole = [lanes(near, n) for n in range(6)]
    grams = [exact(w, w, NT) * (1.0 / 1024) for w in whole]
    diagonal = lax.broadcasted_iota(jnp.int32, (32, 32), 0) == lax.broadcasted_iota(
        jnp.int32, (32, 32), 1
    )
    block_at = lax.axis_index("blk")
    edge = (block_at == 0) | (block_at == lax.axis_size("blk") - 1)
    absent = jnp.where(diagonal, edge.astype(F32), 0.0)
    grams[4] = grams[4] + absent
    grams[5] = grams[5] + absent
    inverse = lower_inverse(jnp.stack(grams))
    before = [jnp.where(even, inverse[4 + n], inverse[2 + n]) for n in range(2)]
    after = [jnp.where(even, inverse[2 + n], inverse[4 + n]) for n in range(2)]
    line = before + [inverse[0], inverse[1]] + after
    right[...] = jnp.zeros((2, 128, 128), F32)
    copy.wait()
    for i in range(2):
        bases[i] = exact(inverse[i], mine[i], NN)
        full = exact(inverse[i], whole[i], NN)
        driven[i] = folded(full, exc[i], NN) * (1.0 / 32)
        left[i] = inverse[i] * (1.0 / 32)
        for k, o in enumerate((-2, -1, 1, 2)):
            at = slice(32 * k, 32 * k + 32)
            right[i, at, at] = line[2 + i + o]


def sum_kernel(parts, left, right, out):
    total = parts[0, 0]
    for g in range(1, 8):
        total = total + parts[g % 2, g // 2]
    for i in range(2):
        value = exact(exact(left[i], total[i], NN), right[i], NT)
        for k in range(4):
            out[i, k] = value[:, 32 * k : 32 * k + 32]


def in_hbm(value):
    return pltpu.with_memory_space_constraint(value, pltpu.HBM)


def in_vmem(value):
    return pltpu.with_memory_space_constraint(value, pltpu.VMEM)


def exchange(first, second):
    size, width = lax.axis_size("blk"), lax.axis_size("grp")

    def pairs(start):
        both = []
        for i in range(start, size - 1, 2):
            turn = width // 2 if i % run_length == run_length - 1 else 0
            for g in range(width):
                here, there = i * width + g, (i + 1) * width + (g ^ turn)
                both += [(here, there), (there, here)]
        return both

    axes = ("blk", "grp")
    got_second = lax.ppermute(second, axes, pairs(1))
    got_first = lax.ppermute(first, axes, pairs(0))
    return got_first, got_second


def over_chips(value):
    return lax.all_to_all(value, "grp", 0, 0, axis_index_groups=chip_groups)


def over_cores(value):
    return lax.all_gather(value, "grp", axis=0, axis_index_groups=core_groups)


def shards(excitation, inverse_self, coupling, neighbour_mask, sketch):
    tests = sketch.transpose(0, 2, 1).reshape(160, 256)
    own, local, first, second = call(
        primary_kernel,
        [(2, 32, 128), (2, 32, 128), (3, 32, 128), (3, 32, 128)],
        hbm=3,
        scratch=[
            pltpu.VMEM((2, 1024, 256), BF16),
            pltpu.VMEM((2, 128, 1024), BF16),
            pltpu.VMEM((160, 256), F32),
            pltpu.SemaphoreType.DMA((5,)),
        ],
    )(in_hbm(excitation), in_hbm(inverse_self), in_hbm(tests))
    got_first, got_second = exchange(first, second)
    pieces = jnp.concatenate([local, got_first, got_second], axis=0)
    same = lax.all_gather(pieces, "grp", axis=0, axis_index_groups=chip_groups)
    other = lax.ppermute(same, "grp", [(g, g ^ 1) for g in range(8)])
    (sources,) = call(
        sources_kernel,
        [(4, 2, 32, 128)],
        scratch=[pltpu.VMEM((8, 8, 32, 128), BF16), pltpu.VMEM((8, 8, 32, 128), BF16)],
    )(neighbour_mask, same, other, coupling)
    whole_sources = over_cores(over_chips(sources))
    (sketched,) = call(sketched_kernel, [(2, 32, 128)])(own, whole_sources, inverse_self)
    got_first, got_second = exchange(sketched, sketched)
    near = lax.all_gather(
        jnp.concatenate([sketched, got_first, got_second], axis=0), "grp", axis=0
    )
    (products,) = call(products_kernel, [(4, 2, 32, 128)])(near, sketched, coupling)
    parts = over_chips(in_vmem(products))
    bases, driven, left, right = call(
        factor_kernel,
        [(2, 32, 128), (2, 32, 256), (2, 32, 32), (2, 128, 128)],
        hbm=1,
        scratch=[pltpu.VMEM((2, 1024, 256), BF16), pltpu.SemaphoreType.DMA],
    )(in_hbm(excitation), near, sketched)
    (reduced,) = call(sum_kernel, [(2, 4, 32, 32)])(over_cores(parts), in_vmem(left), in_vmem(right))
    return bases.transpose(0, 2, 1), reduced, driven


def solution(mesh):
    return jax.shard_map(
        shards,
        mesh=mesh,
        in_specs=(
            P("blk", None, None),
            P("blk", "grp", None),
            P("blk", None, "grp", None),
            P("blk", None),
            P(),
        ),
        out_specs=(P("blk", "grp", None), P("blk", None, None, None), P("blk", None, None)),
        check_vma=False,
    )
```
